32 devices in a mesh: front: 16 (over z, y, x), panel: 2 (over core).
Axes of the slice: x: 2, y: 2, z: 4, core: 2. Of those that a mesh axis runs over, the one named last changes fastest.
Arguments:
- sep_factor: bfloat16 [16384, 1024], P(('front', 'panel')), may hold values from -3 to 3, as said below
- coup_factor: bfloat16 [32768, 1024], P(('front', 'panel')), may hold values from -0.1875 to 0.1875
- coup_list: int32 [16, 16], replicated, may hold values from -1 to 15, as said below
- slot_tiles: int32 [16, 16], replicated, may hold values from 0 to 255, as said below
- anc_tiles: bfloat16 [32768, 128], P('front'), may hold values from -50 to 50
Outputs:
- selected_inverse: float32 [16384, 1024], P(('front', 'panel'))
- variances: float32 [16384], P(('front', 'panel'))
The draws below stay inside these ranges and needn't reach their ends.
Inputs may be any that keep to these rules, and one draw needn't show every extreme that they name: `sep_factor`: each front's block of 1024 rows is lower triangular with a diagonal of 1 or more. `coup_list`: a front's entries name distinct blocks; live entries come first and the rest are -1; every front has 4 or more live entries and some front has 16. `slot_tiles`: every strip id of 0 to 255 appears in exactly one slot; every group holds exactly one strip of each block row.
All inputs are finite; a program needn't handle non-finite values.
Results may differ from the reference program's by a relative error of at most 0.0056.
Values may be sent and summed in bfloat16 or wider, within the bound.
A program may use at most 128 MiB of HBM per device.

```python
import math
import jax
import jax.numpy as jnp
from jax import lax

NS = 1024
BLK = 128
MAXB = 16
NAB = 16
MAXA = 2048
STRIPS = 1
SR = 128
N_FRONT = 16


def slot_layout(key):
    keys = jax.random.split(key, 2)
    strip_count = NAB * N_FRONT
    row_keys = jax.random.split(keys[0], NAB)
    owner = jax.vmap(lambda row_key: jax.random.permutation(row_key, N_FRONT))(row_keys).reshape(-1)
    jitter = jax.random.permutation(keys[1], strip_count)
    order = jnp.argsort(owner * strip_count + jitter, stable=True)
    return order.astype(jnp.int32).reshape(N_FRONT, NAB)


def draw_slot_tiles(key, part):
    return slot_layout(jax.random.fold_in(key, 11))


def draw_anc_tiles(key, part):
    slots = slot_layout(jax.random.fold_in(key, 11)).reshape(-1)
    order_all = NAB * BLK
    noise = jax.random.normal(jax.random.fold_in(key, 12), (order_all, order_all), jnp.float32)
    matrix = (noise + noise.T) * (0.3 / math.sqrt(2.0))
    diagonal = jax.random.uniform(jax.random.fold_in(key, 13), (order_all,), jnp.float32, 1.5, 3.0)
    matrix = matrix + jnp.diag(diagonal)
    matrix = jnp.clip(matrix, -50.0, 50.0)
    strips = matrix.reshape(NAB, STRIPS, SR, NAB, BLK).transpose(0, 3, 1, 2, 4).reshape(NAB * NAB * STRIPS, SR, BLK)
    return strips[slots].reshape(-1, BLK).astype(jnp.bfloat16)


def draw_sep_factor(key, part):
    total_rows = N_FRONT * NS
    noise = jax.random.normal(jax.random.fold_in(key, 21), (total_rows, NS), jnp.float32) * (1.0 / math.sqrt(NS))
    noise = jnp.clip(noise, -1.0, 1.0)
    diagonal = jnp.exp(jax.random.uniform(jax.random.fold_in(key, 22), (total_rows,), jnp.float32, 0.0, math.log(3.0)))
    ratio = jax.random.uniform(jax.random.fold_in(key, 23), (total_rows,), jnp.float32, 0.4, 0.85)
    local_row = jnp.arange(total_rows) % NS
    column = jnp.arange(NS)
    below = local_row[:, None] > column[None, :]
    on_diag = local_row[:, None] == column[None, :]
    next_to = local_row[:, None] == column[None, :] + 1
    result = jnp.where(below & ~next_to, noise, 0.0)
    result = result + jnp.where(on_diag, diagonal[:, None], 0.0)
    result = result + jnp.where(next_to, -(ratio * diagonal)[:, None], 0.0)
    return result.astype(jnp.bfloat16)


def draw_coup_list(key, part):
    keys = jax.random.split(jax.random.fold_in(key, 31), N_FRONT)
    perms = jax.vmap(lambda front_key: jax.random.permutation(front_key, NAB))(keys)[:, :MAXB]
    counts = jax.random.randint(jax.random.fold_in(key, 32), (N_FRONT,), MAXB // 4, MAXB + 1)
    heavy = jax.random.randint(jax.random.fold_in(key, 33), (), 0, N_FRONT)
    counts = jnp.where(jnp.arange(N_FRONT) == heavy, MAXB, counts)
    position = jnp.arange(MAXB)
    return jnp.where(position[None, :] < counts[:, None], perms, -1).astype(jnp.int32)


def level_of(own_key, extent, cuts, low, largest):
    factor_of = 1.0
    for dim, parts in cuts:
        heights = jax.random.uniform(jax.random.fold_in(jax.random.fold_in(own_key, 6), dim), (parts,), jnp.float32, low / len(cuts), largest / len(cuts))
        factor_of = factor_of * jnp.repeat(jnp.exp(heights), extent[dim] // parts).reshape((-1,) + (1,) * (len(extent) - 1 - dim))
    return factor_of


def normal_values(stream_key, dims, spread, reach, shards=(), held_as=jnp.bfloat16):
    values = jax.random.normal(stream_key, dims, jnp.float32) * spread
    if len(shards) > 0:
        values = level_of(stream_key, dims, shards, -0.22, 0.18) * values
    return jnp.clip(values, min=-reach, max=reach).astype(held_as)


def setup_inputs(seed: int = 0) -> dict:
    key_of = jax.random.split(jax.random.key(seed), 6)
    return {
        "sep_factor": draw_sep_factor(jax.random.fold_in(key_of[5], 71), 0),
        "coup_factor": normal_values(key_of[1], (N_FRONT * MAXA, NS), NS ** -0.5, 0.1875, ((0, 32),)),
        "coup_list": draw_coup_list(jax.random.fold_in(key_of[5], 71), 0),
        "slot_tiles": draw_slot_tiles(jax.random.fold_in(key_of[5], 71), 0),
        "anc_tiles": draw_anc_tiles(jax.random.fold_in(key_of[5], 71), 0),
    }


def reference(sep_factor, coup_factor, coup_list, slot_tiles, anc_tiles):
    pool_strips = jnp.zeros((NAB * NAB * STRIPS, SR, BLK), anc_tiles.dtype)
    pool_strips = pool_strips.at[slot_tiles.reshape(-1)].set(anc_tiles.reshape(-1, SR, BLK))
    pool_tiles = pool_strips.reshape(NAB, NAB, BLK, BLK)
    identity = jnp.eye(NS, dtype=jnp.float32)

    def per_front(front_index):
        lower_full = lax.dynamic_slice_in_dim(sep_factor, front_index * NS, NS, 0).astype(jnp.float32)
        inverse = lax.linalg.triangular_solve(lower_full, identity, left_side=True, lower=True)
        coupling = lax.dynamic_slice_in_dim(coup_factor, front_index * MAXA, MAXA, 0)
        blocks = coup_list[front_index]
        live_blocks = blocks >= 0
        safe_blocks = jnp.where(live_blocks, blocks, 0)
        row_live = jnp.repeat(live_blocks, BLK)
        coupling = jnp.where(row_live[:, None], coupling, jnp.zeros_like(coupling))
        wide_full = jnp.dot(coupling.astype(jnp.float32), inverse.astype(jnp.bfloat16).astype(jnp.float32), preferred_element_type=jnp.float32).astype(jnp.bfloat16)
        picked = pool_tiles[safe_blocks][:, safe_blocks]
        both_live = live_blocks[:, None] & live_blocks[None, :]
        picked = jnp.where(both_live[:, :, None, None], picked, jnp.zeros_like(picked))
        sigma_pair = picked.transpose(0, 2, 1, 3).reshape(MAXA, MAXA)
        carried = jnp.dot(sigma_pair.astype(jnp.float32), wide_full.astype(jnp.float32), preferred_element_type=jnp.float32).astype(jnp.bfloat16)
        product = jnp.dot(wide_full.T.astype(jnp.float32), carried.astype(jnp.float32), preferred_element_type=jnp.float32)
        inverse_square = jnp.dot(inverse.T, inverse, precision=lax.Precision.HIGHEST)
        selected = inverse_square + product
        return (selected, jnp.diagonal(selected))
    selected_all, variances = lax.map(per_front, jnp.arange(N_FRONT, dtype=jnp.int32))
    return (selected_all.reshape(N_FRONT * NS, NS), variances.reshape(N_FRONT * NS))
```

```python
import functools

import jax
import jax.numpy as jnp
from jax import lax
from jax.experimental import pallas as pl
from jax.experimental.pallas import tpu as pltpu
from jax.sharding import PartitionSpec as P

BF = jnp.bfloat16
F32 = jnp.float32
DIAG = 128


def mm(a, b):
    return jnp.dot(a, b, preferred_element_type=F32)


def split(x):
    hi = x.astype(BF)
    return hi, (x - hi.astype(F32)).astype(BF)


def invert(lmat, xh, xl, xd):
    n = lmat.shape[0]
    blocks = n // DIAG
    row = lax.broadcasted_iota(jnp.int32, (DIAG, DIAG), 0)
    col = lax.broadcasted_iota(jnp.int32, (DIAG, DIAG), 1)
    eye = row == col
    xh[...] = jnp.zeros_like(xh)
    xl[...] = jnp.zeros_like(xl)
    for b in range(blocks):
        span = pl.ds(b * DIAG, DIAG)
        block = lmat[span, span].astype(F32)
        xd[b] = jnp.where(eye, 1.0 / jnp.where(eye, block, 1.0), 0.0)

    def level(step, carry):
        mask = (
            ((row >> (step + 1)) == (col >> (step + 1)))
            & (((row >> step) & 1) == 1)
            & (((col >> step) & 1) == 0)
        )
        for b in range(blocks):
            span = pl.ds(b * DIAG, DIAG)
            x = xd[b]
            hi, lo = split(x)
            below = jnp.where(mask, lmat[span, span].astype(F32), 0.0).astype(BF)
            y = mm(below, jnp.concatenate([hi, lo], axis=1))
            yhi, ylo = split(y[:, :DIAG] + y[:, DIAG:])
            z = mm(jnp.concatenate([hi, lo], axis=0), jnp.concatenate([yhi, ylo], axis=1))
            z = (z[:DIAG, :DIAG] + z[:DIAG, DIAG:]) + (z[DIAG:, :DIAG] + z[DIAG:, DIAG:])
            xd[b] = x - z
        return carry

    levels = DIAG.bit_length() - 1
    lax.fori_loop(0, levels, level, 0)
    for b in range(blocks):
        span = pl.ds(b * DIAG, DIAG)
        xh[span, span], xl[span, span] = split(xd[b])
    size = DIAG
    while size < n:
        for start in range(0, n, 2 * size):
            top, low = pl.ds(start, size), pl.ds(start + size, size)
            below = lmat[low, top]
            thi, tlo = split(mm(below, xh[top, top]) + mm(below, xl[top, top]))
            z = mm(xh[low, low], thi) + (mm(xh[low, low], tlo) + mm(xl[low, low], thi))
            xh[low, top], xl[low, top] = split(-z)
        size *= 2


def first_kernel(sep_ref, sep_other, coup_ref, coup_other, live_ref, inv_ref, wide_ref, lmat, xl, xd):
    me = lax.axis_index("panel")
    half = sep_ref.shape[0]
    lmat[pl.ds(pl.multiple_of(me * half, half), half), :] = sep_ref[...]
    lmat[pl.ds(pl.multiple_of((1 - me) * half, half), half), :] = sep_other[...]
    invert(lmat, inv_ref, xl, xd)
    rows = coup_ref.shape[0]
    chunk = min(512, rows)
    columns = pl.ds(pl.multiple_of(me * half, half), half)

    @pl.loop(0, rows // chunk)
    def _(i):
        for source, base in ((coup_ref, 0), (coup_other, rows)):
            take = pl.ds(pl.multiple_of(i * chunk, chunk), chunk)
            put = pl.ds(pl.multiple_of(base + i * chunk, chunk), chunk)
            w = mm(source[take, :], inv_ref[:, columns])
            wide_ref[put, :] = jnp.where(live_ref[put, :] > 0, w, 0.0).astype(BF)


def last_kernel(where_ref, wide_ref, wide_other, inv_ref, pool_ref, out_ref, var_ref, sigma, sem):
    me = lax.axis_index("panel")
    rows, half = wide_ref.shape
    edge = pool_ref.shape[1]
    width = inv_ref.shape[1]
    strips = where_ref.shape[0]
    strip_rows = rows * rows // (strips * edge)
    across = rows // edge

    def tile_copy(k):
        source = pl.ds(pl.multiple_of(where_ref[k] * strip_rows, strip_rows), strip_rows)
        down = pl.multiple_of((k // across) * strip_rows, strip_rows)
        over = pl.multiple_of((k % across) * edge, edge)
        return pltpu.make_async_copy(
            pool_ref.at[source, :], sigma.at[pl.ds(down, strip_rows), pl.ds(over, edge)], sem
        )

    @pl.loop(0, strips)
    def _(k):
        tile_copy(k).start()

    mine = pl.ds(pl.multiple_of(me * half, half), half)
    other = pl.ds(pl.multiple_of((1 - me) * half, half), half)
    contract = (((0,), (0,)), ((), ()))

    def tmm(a, b):
        return lax.dot_general(a, b, contract, preferred_element_type=F32)

    out_ref[...] = tmm(inv_ref[:, mine], inv_ref[...])
    pltpu.make_async_copy(pool_ref.at[pl.ds(0, rows * rows // edge), :], pool_ref.at[pl.ds(0, rows * rows // edge), :], sem).wait()
    chunk = rows // 4

    @pl.loop(0, 4)
    def _(i):
        take = pl.ds(pl.multiple_of(i * chunk, chunk), chunk)
        swapped = pl.ds(pl.multiple_of(((i + 2) % 4) * chunk, chunk), chunk)
        carried = mm(sigma[take, :], wide_ref[...]).astype(BF)
        out_ref[:, mine] += tmm(carried, wide_ref[take, :])
        out_ref[:, other] += tmm(carried, wide_other[swapped, :])

    block = out_ref[:, mine]
    row = lax.broadcasted_iota(jnp.int32, (half, half), 0)
    col = lax.broadcasted_iota(jnp.int32, (half, half), 1)
    var_ref[...] = jnp.sum(jnp.where(row == col, block, 0.0), axis=0, keepdims=True)


def on_device(sep_factor, coup_factor, coup_list, slot_tiles, anc_tiles):
    panels = lax.axis_size("panel")
    groups = lax.axis_size("front")
    me = lax.axis_index("panel")
    my_group = lax.axis_index("front")
    half, width = sep_factor.shape
    edge = anc_tiles.shape[1]
    slots = slot_tiles.shape[1]
    strip_rows = anc_tiles.shape[0] // slots
    strip_count = edge // strip_rows
    list_width = coup_list.shape[1]
    row_blocks = list_width // panels
    rows = list_width * edge
    swap = [(0, 1), (1, 0)]
    vmem = pl.BlockSpec(memory_space=pltpu.VMEM)

    part = anc_tiles.shape[0] // panels
    pool = lax.all_gather(
        lax.dynamic_slice_in_dim(anc_tiles, me * part, part), ("front", "panel"), axis=0, tiled=True
    )
    sep_other = lax.ppermute(sep_factor, "panel", swap)
    coup_other = lax.ppermute(coup_factor, "panel", swap)

    own_list = coup_list[my_group]
    own_list = jnp.where(me == 0, own_list, jnp.roll(own_list, -row_blocks))
    live = jnp.repeat((own_list >= 0).astype(F32), edge)[:, None]
    blocks = jnp.maximum(own_list, 0)
    wanted = (
        blocks[:, None, None] * groups
        + jnp.arange(strip_count, dtype=jnp.int32)[None, :, None]
        + blocks[None, None, :] * strip_count
    ).reshape(-1)
    flat = slot_tiles.reshape(-1)
    place = jnp.sum(
        jnp.where(
            wanted[:, None] == flat[None, :], jnp.arange(flat.shape[0], dtype=jnp.int32)[None, :], 0
        ),
        axis=1,
    )

    inverse, wide = pl.pallas_call(
        first_kernel,
        out_shape=(
            jax.ShapeDtypeStruct((width, width), BF),
            jax.ShapeDtypeStruct((rows, half), BF),
        ),
        in_specs=[vmem] * 5,
        out_specs=[vmem] * 2,
        scratch_shapes=[
            pltpu.VMEM((width, width), BF),
            pltpu.VMEM((width, width), BF),
            pltpu.VMEM((width // DIAG, DIAG, DIAG), F32),
        ],
        compiler_params=pltpu.CompilerParams(vmem_limit_bytes=48 << 20),
        cost_estimate=pl.CostEstimate(flops=20 * 10**9, bytes_accessed=12 << 20, transcendentals=0),
    )(sep_factor, sep_other, coup_factor, coup_other, live)
    wide_other = lax.ppermute(wide, "panel", swap)
    selected, variances = pl.pallas_call(
        last_kernel,
        out_shape=(
            jax.ShapeDtypeStruct((half, width), F32),
            jax.ShapeDtypeStruct((1, half), F32),
        ),
        in_specs=[pl.BlockSpec(memory_space=pltpu.SMEM), vmem, vmem, vmem, pl.BlockSpec(memory_space=pl.ANY)],
        out_specs=[vmem] * 2,
        scratch_shapes=[pltpu.VMEM((rows, rows), BF), pltpu.SemaphoreType.DMA],
        compiler_params=pltpu.CompilerParams(vmem_limit_bytes=48 << 20),
    )(place, wide, wide_other, inverse, pool)
    return selected, variances.reshape(half)


def solution(mesh):
    placed = (P(("front", "panel"), None), P(("front", "panel"), None), P(), P(), P("front", None))
    return jax.shard_map(
        on_device,
        mesh=mesh,
        in_specs=placed,
        out_specs=(P(("front", "panel"), None), P(("front", "panel"))),
        check_vma=False,
    )
```

```python
import functools

import jax
import jax.numpy as jnp
from jax import lax
from jax.experimental import pallas as pl
from jax.experimental.pallas import tpu as pltpu
from jax.sharding import PartitionSpec as P

BF = jnp.bfloat16
F32 = jnp.float32
DIAG = 128
MESH = pl.DeviceIdType.MESH


def mm(a, b):
    return jnp.dot(a, b, preferred_element_type=F32)


def split(x):
    hi = x.astype(BF)
    return hi, (x - hi.astype(F32)).astype(BF)


def flip(index, mask):
    bit = 1
    while bit <= mask:
        if mask & bit:
            index = index + bit * (1 - 2 * ((index // bit) % 2))
        bit *= 2
    return index


def first_kernel(
    depth,
    sep_ref,
    coup_ref,
    live_ref,
    anc_ref,
    inv_ref,
    wide_ref,
    wide_other,
    square_ref,
    pool_ref,
    lmat,
    sep_other,
    coup_other,
    xl,
    xd,
    panel_send,
    panel_recv,
    z_recv,
    x_recv,
    y_recv,
    first_recv,
    second_recv,
    share_recv,
    out_send,
    local_sem,
):
    me = lax.axis_index("panel")
    group = lax.axis_index("front")
    layer, spot = group // 4, group % 4
    half, n = sep_ref.shape[0], sep_ref.shape[1]
    slab = anc_ref.shape[0]
    part = slab // 2
    partner = (group, 1 - me)
    beside = (layer * 4 + flip(spot, 1), me)
    behind = (layer * 4 + flip(spot, 2), me)
    peers = [(flip(layer, k) * 4 + spot, me) for k in range(1, depth)]

    barrier = pltpu.get_barrier_semaphore()
    for device in [partner, beside, behind] + peers:
        pl.semaphore_signal(barrier, inc=1, device_id=device, device_id_type=MESH)
    pl.semaphore_wait(barrier, 2 + depth)

    def remote(source, target, send, recv, device):
        return pltpu.make_async_remote_copy(
            src_ref=source, dst_ref=target, send_sem=send, recv_sem=recv, device_id=device, device_id_type=MESH
        )

    def place(k, mask, low=0, size=part):
        owner = flip(layer, k) * 4 + flip(spot, mask)
        start = pl.multiple_of(owner * slab + me * part + low, part // 2)
        return pool_ref.at[pl.ds(start, size), :]

    def push(source, target, recv, device):
        remote(source, target, out_send, recv, device).start()

    def arrived(target, recv):
        remote(target, target, out_send, recv, partner).wait_recv()

    own = anc_ref.at[pl.ds(pl.multiple_of(me * part, part), part), :]

    def open_block(k):
        source = own if k == 0 else place(k, 0)
        if k > 0:
            arrived(source, z_recv.at[k])
        push(source, place(k, 0), x_recv.at[k], beside)
        push(source, place(k, 0), y_recv.at[k], behind)
        if k > 0:
            push(source, source, share_recv, partner)

    def relay(k):
        piece = part // 2
        arrived(place(k, 1), x_recv.at[k])
        push(place(k, 1, piece, piece), place(k, 1, piece, piece), second_recv.at[k], behind)
        arrived(place(k, 2), y_recv.at[k])
        push(place(k, 2, 0, piece), place(k, 2, 0, piece), first_recv.at[k], beside)
        push(place(k, 1), place(k, 1), share_recv, partner)
        push(place(k, 2), place(k, 2), share_recv, partner)

    def finish(k):
        piece = part // 2
        arrived(place(k, 3, 0, piece), first_recv.at[k])
        arrived(place(k, 3, piece, piece), second_recv.at[k])
        push(place(k, 3), place(k, 3), share_recv, partner)

    def stage(k):
        if k < depth:
            open_block(k)
        if 1 <= k <= depth:
            relay(k - 1)
        if 2 <= k <= depth + 1:
            finish(k - 2)

    sep_copy = remote(sep_ref, sep_other, panel_send.at[0], panel_recv.at[0], partner)
    coup_copy = remote(coup_ref, coup_other, panel_send.at[1], panel_recv.at[1], partner)
    wide_copy = remote(wide_ref, wide_other, panel_send.at[2], panel_recv.at[2], partner)
    sep_copy.start()
    for k in range(1, depth):
        push(own, place(0, 0), z_recv.at[k], peers[k - 1])
        if k == 1:
            stage(0)
    coup_copy.start()
    keep = pltpu.make_async_copy(
        anc_ref, pool_ref.at[pl.ds(pl.multiple_of(group * slab, slab), slab), :], local_sem
    )
    keep.start()

    lmat[pl.ds(pl.multiple_of(me * half, half), half), :] = sep_ref[...]
    inv_ref[...] = jnp.zeros_like(inv_ref)
    xl[...] = jnp.zeros_like(xl)
    sep_copy.wait_recv()
    lmat[pl.ds(pl.multiple_of((1 - me) * half, half), half), :] = sep_other[...]

    blocks = n // DIAG
    row = lax.broadcasted_iota(jnp.int32, (DIAG, DIAG), 0)
    col = lax.broadcasted_iota(jnp.int32, (DIAG, DIAG), 1)
    eye = row == col
    for b in range(blocks):
        span = pl.ds(b * DIAG, DIAG)
        block = lmat[span, span].astype(F32)
        xd[b] = jnp.where(eye, 1.0 / jnp.where(eye, block, 1.0), 0.0)

    def level(step, carry):
        mask = (
            ((row >> (step + 1)) == (col >> (step + 1)))
            & (((row >> step) & 1) == 1)
            & (((col >> step) & 1) == 0)
        )
        for b in range(blocks):
            span = pl.ds(b * DIAG, DIAG)
            x = xd[b]
            hi, lo = split(x)
            below = jnp.where(mask, lmat[span, span].astype(F32), 0.0).astype(BF)
            y = mm(below, jnp.concatenate([hi, lo], axis=1))
            yhi, ylo = split(y[:, :DIAG] + y[:, DIAG:])
            t = mm(jnp.concatenate([hi, lo], axis=0), jnp.concatenate([yhi, ylo], axis=1))
            t = (t[:DIAG, :DIAG] + t[:DIAG, DIAG:]) + (t[DIAG:, :DIAG] + t[DIAG:, DIAG:])
            xd[b] = x - t
        return carry

    levels = DIAG.bit_length() - 1
    lax.fori_loop(0, levels // 2, level, 0)
    stage(1)
    lax.fori_loop(levels // 2, levels, level, 0)
    for b in range(blocks):
        span = pl.ds(b * DIAG, DIAG)
        inv_ref[span, span], xl[span, span] = split(xd[b])
    size = DIAG
    while size < n:
        for start in range(0, n, 2 * size):
            top, low = pl.ds(start, size), pl.ds(start + size, size)
            below = lmat[low, top]
            thi, tlo = split(mm(below, inv_ref[top, top]) + mm(below, xl[top, top]))
            t = mm(inv_ref[low, low], thi) + (mm(inv_ref[low, low], tlo) + mm(xl[low, low], thi))
            inv_ref[low, top], xl[low, top] = split(-t)
        size *= 2
    stage(2)

    rows = coup_ref.shape[0]
    chunk = min(512, rows)
    columns = pl.ds(pl.multiple_of(me * half, half), half)
    coup_copy.wait_recv()

    @pl.loop(0, rows // chunk)
    def _(i):
        for source, base in ((coup_ref, 0), (coup_other, rows)):
            take = pl.ds(pl.multiple_of(i * chunk, chunk), chunk)
            put = pl.ds(pl.multiple_of(base + i * chunk, chunk), chunk)
            w = mm(source[take, :], inv_ref[:, columns])
            wide_ref[put, :] = jnp.where(live_ref[put, :] > 0, w, 0.0).astype(BF)

    stage(3)
    wide_copy.start()

    @pl.loop(0, n // 256)
    def _(i):
        take = pl.ds(pl.multiple_of(i * 256, 256), 256)
        square_ref[:, take] = lax.dot_general(
            inv_ref[:, columns], inv_ref[:, take], (((0,), (0,)), ((), ())), preferred_element_type=F32
        )

    for k in range(4, depth + 2):
        stage(k)

    total = 4 * depth - 1
    shared = pool_ref.at[pl.ds(0, total * part), :]
    remote(shared, shared, out_send, share_recv, partner).wait_recv()
    sent = pool_ref.at[pl.ds(0, (2 * total) * part), :]
    remote(sent, sent, out_send, share_recv, partner).wait_send()
    keep.wait()
    sep_copy.wait_send()
    coup_copy.wait_send()
    wide_copy.wait()


def last_kernel(where_ref, wide_ref, wide_other, square_ref, pool_ref, out_ref, var_ref, sigma, sem):
    me = lax.axis_index("panel")
    rows, half = wide_ref.shape
    edge = pool_ref.shape[1]
    strips = where_ref.shape[0]
    strip_rows = rows * rows // (strips * edge)
    across = rows // edge
    chunks = sem.shape[0]
    chunk = rows // chunks

    @pl.loop(0, strips)
    def _(k):
        source = pl.ds(pl.multiple_of(where_ref[k] * strip_rows, strip_rows), strip_rows)
        down = pl.multiple_of((k // across) * strip_rows, strip_rows)
        over = pl.multiple_of((k % across) * edge, edge)
        pltpu.make_async_copy(
            pool_ref.at[source, :],
            sigma.at[pl.ds(down, strip_rows), pl.ds(over, edge)],
            sem.at[k // (strips // chunks)],
        ).start()

    mine = pl.ds(pl.multiple_of(me * half, half), half)
    other = pl.ds(pl.multiple_of((1 - me) * half, half), half)

    def tmm(a, b):
        return lax.dot_general(a, b, (((0,), (0,)), ((), ())), preferred_element_type=F32)

    out_ref[...] = square_ref[...]

    @pl.loop(0, chunks)
    def _(i):
        take = pl.ds(pl.multiple_of(i * chunk, chunk), chunk)
        turned = ((i + chunks // 2) % chunks) * chunk
        swapped = pl.ds(pl.multiple_of(turned, chunk), chunk)
        pltpu.make_async_copy(sigma.at[take, :], sigma.at[take, :], sem.at[i]).wait()
        carried = mm(sigma[take, :], wide_ref[...]).astype(BF)
        out_ref[:, mine] += tmm(carried, wide_ref[take, :])
        out_ref[:, other] += tmm(carried, wide_other[swapped, :])

    block = out_ref[:, mine]
    row = lax.broadcasted_iota(jnp.int32, (half, half), 0)
    col = lax.broadcasted_iota(jnp.int32, (half, half), 1)
    var_ref[...] = jnp.sum(jnp.where(row == col, block, 0.0), axis=0, keepdims=True)


def on_device(sep_factor, coup_factor, coup_list, slot_tiles, anc_tiles):
    panels = lax.axis_size("panel")
    groups = lax.axis_size("front")
    me = lax.axis_index("panel")
    my_group = lax.axis_index("front")
    half, width = sep_factor.shape
    edge = anc_tiles.shape[1]
    slots = slot_tiles.shape[1]
    strip_rows = anc_tiles.shape[0] // slots
    strip_count = edge // strip_rows
    list_width = coup_list.shape[1]
    row_blocks = list_width // panels
    rows = list_width * edge
    vmem = pl.BlockSpec(memory_space=pltpu.VMEM)
    hbm = pl.BlockSpec(memory_space=pl.ANY)

    own_list = coup_list[my_group]
    own_list = jnp.where(me == 0, own_list, jnp.roll(own_list, -row_blocks))
    live = jnp.repeat((own_list >= 0).astype(F32), edge)[:, None]
    blocks = jnp.maximum(own_list, 0)
    wanted = (
        blocks[:, None, None] * groups
        + jnp.arange(strip_count, dtype=jnp.int32)[None, :, None]
        + blocks[None, None, :] * strip_count
    ).reshape(-1)
    flat = slot_tiles.reshape(-1)
    place = jnp.sum(
        jnp.where(
            wanted[:, None] == flat[None, :], jnp.arange(flat.shape[0], dtype=jnp.int32)[None, :], 0
        ),
        axis=1,
    )

    depth = groups // 4
    dma = pltpu.SemaphoreType.DMA
    _, wide, wide_other, square, pool = pl.pallas_call(
        functools.partial(first_kernel, depth),
        out_shape=(
            jax.ShapeDtypeStruct((width, width), BF),
            jax.ShapeDtypeStruct((rows, half), BF),
            jax.ShapeDtypeStruct((rows, half), BF),
            jax.ShapeDtypeStruct((half, width), F32),
            jax.ShapeDtypeStruct((groups * anc_tiles.shape[0], edge), BF),
        ),
        in_specs=[vmem] * 3 + [hbm],
        out_specs=[vmem] * 4 + [hbm],
        scratch_shapes=[
            pltpu.VMEM((width, width), BF),
            pltpu.VMEM((half, width), BF),
            pltpu.VMEM((rows // panels, width), BF),
            pltpu.VMEM((width, width), BF),
            pltpu.VMEM((width // DIAG, DIAG, DIAG), F32),
            dma((3,)),
            dma((3,)),
            dma((depth,)),
            dma((depth,)),
            dma((depth,)),
            dma((depth,)),
            dma((depth,)),
            dma,
            dma,
            dma,
        ],
        compiler_params=pltpu.CompilerParams(
            vmem_limit_bytes=48 << 20, collective_id=0, has_side_effects=True
        ),
    )(sep_factor, coup_factor, live, anc_tiles)
    selected, variances = pl.pallas_call(
        last_kernel,
        out_shape=(
            jax.ShapeDtypeStruct((half, width), F32),
            jax.ShapeDtypeStruct((1, half), F32),
        ),
        in_specs=[pl.BlockSpec(memory_space=pltpu.SMEM), vmem, vmem, vmem, hbm],
        out_specs=[vmem] * 2,
        scratch_shapes=[pltpu.VMEM((rows, rows), BF), dma((4,))],
        compiler_params=pltpu.CompilerParams(vmem_limit_bytes=48 << 20),
    )(place, wide, wide_other, square, pool)
    return selected, variances.reshape(half)


def solution(mesh):
    placed = (P(("front", "panel"), None), P(("front", "panel"), None), P(), P(), P("front", None))
    return jax.shard_map(
        on_device,
        mesh=mesh,
        in_specs=placed,
        out_specs=(P(("front", "panel"), None), P(("front", "panel"))),
        check_vma=False,
    )
```

```python
import functools

import jax
import jax.numpy as jnp
from jax import lax
from jax.experimental import pallas as pl
from jax.experimental.pallas import tpu as pltpu
from jax.sharding import PartitionSpec as P

BF = jnp.bfloat16
F32 = jnp.float32
DIAG = 128
MESH = pl.DeviceIdType.MESH


def mm(a, b):
    return jnp.dot(a, b, preferred_element_type=F32)


def split(x):
    hi = x.astype(BF)
    return hi, (x - hi.astype(F32)).astype(BF)


def flip(index, mask):
    bit = 1
    while bit <= mask:
        if mask & bit:
            index = index + bit * (1 - 2 * ((index // bit) % 2))
        bit *= 2
    return index


def first_kernel(
    depth,
    sep_ref,
    coup_ref,
    anc_ref,
    wide_out,
    wide_other,
    square_out,
    pool_ref,
    inv_ref,
    wide_ref,
    square_ref,
    lmat,
    coup_all,
    xl,
    xd,
    panel_send,
    panel_recv,
    z_recv,
    x_recv,
    y_recv,
    first_recv,
    second_recv,
    share_recv,
    out_send,
    local_sem,
):
    me = lax.axis_index("panel")
    group = lax.axis_index("front")
    layer, spot = group // 4, group % 4
    half, n = sep_ref.shape[0], sep_ref.shape[1]
    slab = anc_ref.shape[0]
    part = slab // 2
    partner = (group, 1 - me)
    beside = (layer * 4 + flip(spot, 1), me)
    behind = (layer * 4 + flip(spot, 2), me)
    peers = [(flip(layer, k) * 4 + spot, me) for k in range(1, depth)]

    barrier = pltpu.get_barrier_semaphore()
    for device in [partner, beside, behind] + peers:
        pl.semaphore_signal(barrier, inc=1, device_id=device, device_id_type=MESH)
    pl.semaphore_wait(barrier, 2 + depth)

    def remote(source, target, send, recv, device):
        return pltpu.make_async_remote_copy(
            src_ref=source, dst_ref=target, send_sem=send, recv_sem=recv, device_id=device, device_id_type=MESH
        )

    def place(k, mask, low=0, size=part):
        owner = flip(layer, k) * 4 + flip(spot, mask)
        start = pl.multiple_of(owner * slab + me * part + low, part // 2)
        return pool_ref.at[pl.ds(start, size), :]

    def push(source, target, recv, device):
        remote(source, target, out_send, recv, device).start()

    def arrived(target, recv):
        remote(target, target, out_send, recv, partner).wait_recv()

    own = anc_ref.at[pl.ds(pl.multiple_of(me * part, part), part), :]

    def open_block(k):
        source = own if k == 0 else place(k, 0)
        if k > 0:
            arrived(source, z_recv.at[k])
        push(source, place(k, 0), x_recv.at[k], beside)
        push(source, place(k, 0), y_recv.at[k], behind)
        if k > 0:
            push(source, source, share_recv, partner)

    def relay(k):
        piece = part // 2
        arrived(place(k, 1), x_recv.at[k])
        push(place(k, 1, piece, piece), place(k, 1, piece, piece), second_recv.at[k], behind)
        arrived(place(k, 2), y_recv.at[k])
        push(place(k, 2, 0, piece), place(k, 2, 0, piece), first_recv.at[k], beside)
        push(place(k, 1), place(k, 1), share_recv, partner)
        push(place(k, 2), place(k, 2), share_recv, partner)

    def finish(k):
        piece = part // 2
        arrived(place(k, 3, 0, piece), first_recv.at[k])
        arrived(place(k, 3, piece, piece), second_recv.at[k])
        push(place(k, 3), place(k, 3), share_recv, partner)

    def stage(k):
        if 2 <= k <= depth + 1:
            finish(k - 2)
        if 1 <= k <= depth:
            relay(k - 1)
        if k < depth:
            open_block(k)

    rows = coup_ref.shape[0]
    upper = pl.ds(pl.multiple_of(me * half, half), half)
    sep_copy = remote(sep_ref, lmat.at[upper, :], panel_send.at[0], panel_recv.at[0], partner)
    coup_copy = remote(coup_ref, coup_all.at[pl.ds(rows, rows), :], panel_send.at[1], panel_recv.at[1], partner)
    wide_copy = remote(wide_ref, wide_other, panel_send.at[2], panel_recv.at[2], partner)
    sep_keep = pltpu.make_async_copy(sep_ref, lmat.at[upper, :], local_sem.at[0])
    sep_copy.start()
    for k in range(1, depth):
        push(own, place(0, 0), z_recv.at[k], peers[k - 1])
        if k == 1:
            stage(0)
    coup_copy.start()
    sep_keep.start()
    coup_keep = pltpu.make_async_copy(coup_ref, coup_all.at[pl.ds(0, rows), :], local_sem.at[1])
    coup_keep.start()
    keep = pltpu.make_async_copy(
        anc_ref, pool_ref.at[pl.ds(pl.multiple_of(group * slab, slab), slab), :], local_sem.at[2]
    )
    keep.start()

    inv_ref[...] = jnp.zeros_like(inv_ref)
    xl[...] = jnp.zeros_like(xl)
    sep_keep.wait()
    remote(sep_ref, lmat.at[pl.ds(pl.multiple_of((1 - me) * half, half), half), :], panel_send.at[0], panel_recv.at[0], partner).wait_recv()

    blocks = n // DIAG
    row = lax.broadcasted_iota(jnp.int32, (DIAG, DIAG), 0)
    col = lax.broadcasted_iota(jnp.int32, (DIAG, DIAG), 1)
    eye = row == col
    for b in range(blocks):
        span = pl.ds(b * DIAG, DIAG)
        block = lmat[span, span].astype(F32)
        xd[b] = jnp.where(eye, 1.0 / jnp.where(eye, block, 1.0), 0.0)

    def level(step, carry):
        mask = (
            ((row >> (step + 1)) == (col >> (step + 1)))
            & (((row >> step) & 1) == 1)
            & (((col >> step) & 1) == 0)
        )
        for b in range(blocks):
            span = pl.ds(b * DIAG, DIAG)
            x = xd[b]
            hi, lo = split(x)
            below = jnp.where(mask, lmat[span, span].astype(F32), 0.0).astype(BF)
            y = mm(below, jnp.concatenate([hi, lo], axis=1))
            yhi, ylo = split(y[:, :DIAG] + y[:, DIAG:])
            t = mm(jnp.concatenate([hi, lo], axis=0), jnp.concatenate([yhi, ylo], axis=1))
            t = (t[:DIAG, :DIAG] + t[:DIAG, DIAG:]) + (t[DIAG:, :DIAG] + t[DIAG:, DIAG:])
            xd[b] = x - t
        return carry

    levels = DIAG.bit_length() - 1
    lax.fori_loop(0, levels // 2, level, 0)
    stage(1)
    lax.fori_loop(levels // 2, levels, level, 0)
    for b in range(blocks):
        span = pl.ds(b * DIAG, DIAG)
        inv_ref[span, span], xl[span, span] = split(xd[b])
    size = DIAG
    while size < n:
        for start in range(0, n, 2 * size):
            top, low = pl.ds(start, size), pl.ds(start + size, size)
            below = lmat[low, top]
            thi, tlo = split(mm(below, inv_ref[top, top]) + mm(below, xl[top, top]))
            t = mm(inv_ref[low, low], thi) + (mm(inv_ref[low, low], tlo) + mm(xl[low, low], thi))
            inv_ref[low, top], xl[low, top] = split(-t)
        size *= 2
    stage(2)

    chunk = min(512, rows)
    columns = pl.ds(pl.multiple_of(me * half, half), half)
    coup_keep.wait()
    coup_copy.wait_recv()

    @pl.loop(0, 2 * rows // chunk)
    def _(i):
        take = pl.ds(pl.multiple_of(i * chunk, chunk), chunk)
        wide_ref[take, :] = mm(coup_all[take, :], inv_ref[:, columns]).astype(BF)

    stage(3)
    wide_copy.start()
    wide_keep = pltpu.make_async_copy(wide_ref, wide_out, local_sem.at[3])
    wide_keep.start()
    strip = pool_ref.shape[0] - 4 * depth * slab
    blank = pltpu.make_async_copy(
        inv_ref.at[pl.ds(0, strip), pl.ds(n - DIAG, DIAG)], pool_ref.at[pl.ds(4 * depth * slab, strip), :], local_sem.at[4]
    )
    blank.start()

    @pl.loop(0, n // 256)
    def _(i):
        take = pl.ds(pl.multiple_of(i * 256, 256), 256)
        square_ref[:, take] = lax.dot_general(
            inv_ref[:, columns], inv_ref[:, take], (((0,), (0,)), ((), ())), preferred_element_type=F32
        )

    square_keep = pltpu.make_async_copy(square_ref, square_out, local_sem.at[5])
    square_keep.start()
    for k in range(4, depth + 2):
        stage(k)

    total = 4 * depth - 1
    shared = pool_ref.at[pl.ds(0, total * part), :]
    remote(shared, shared, out_send, share_recv, partner).wait_recv()
    sent = pool_ref.at[pl.ds(0, (2 * total) * part), :]
    remote(sent, sent, out_send, share_recv, partner).wait_send()
    for copy in (keep, wide_keep, blank, square_keep):
        copy.wait()
    sep_copy.wait_send()
    coup_copy.wait_send()
    wide_copy.wait()


def last_kernel(
    list_ref,
    slot_ref,
    wide_in,
    other_in,
    square_in,
    pool_ref,
    out_ref,
    var_ref,
    sigma,
    wide,
    wide_other,
    carried,
    out,
    place,
    tile_sem,
    load_sem,
    store_sem,
):
    me = lax.axis_index("panel")
    group = lax.axis_index("front")
    rows, half = wide.shape
    edge = pool_ref.shape[1]
    groups, slots = slot_ref.shape
    total = groups * slots
    strip_rows = rows * rows // (total * edge)
    strip_count = edge // strip_rows
    across = rows // edge
    chunks = tile_sem.shape[0]
    chunk = rows // chunks
    low, high = pl.ds(0, rows // 2), pl.ds(rows // 2, rows // 2)

    load_wide = pltpu.make_async_copy(wide_in, wide, load_sem.at[0])
    load_low = pltpu.make_async_copy(other_in.at[high, :], wide_other.at[low, :], load_sem.at[1])
    load_high = pltpu.make_async_copy(other_in.at[low, :], wide_other.at[high, :], load_sem.at[2])
    load_square = pltpu.make_async_copy(square_in, out, load_sem.at[3])
    load_wide.start()

    @pl.loop(0, groups)
    def _(g):
        for s in range(slots):
            place[slot_ref[g, s]] = g * slots + s

    def block(i):
        return list_ref[group, (i + me * (across // 2)) % across]

    def fetch(i):
        a = block(i)
        for j in range(across):
            b = block(j)
            live = (a >= 0) & (b >= 0)
            for q in range(strip_count):
                at = place[jnp.where(live, a * groups + b * strip_count + q, 0)]
                source = pl.multiple_of(jnp.where(live, at, total) * strip_rows, strip_rows)
                down = pl.multiple_of(i * edge + q * strip_rows, strip_rows)
                pltpu.make_async_copy(
                    pool_ref.at[pl.ds(source, strip_rows), :],
                    sigma.at[pl.ds(down, strip_rows), pl.ds(j * edge, edge)],
                    tile_sem.at[i // (across // chunks)],
                ).start()

    pl.loop(0, across)(fetch)
    load_low.start()
    load_high.start()
    load_square.start()
    load_wide.wait()

    @pl.loop(0, chunks)
    def _(i):
        take = pl.ds(pl.multiple_of(i * chunk, chunk), chunk)
        pltpu.make_async_copy(sigma.at[take, :], sigma.at[take, :], tile_sem.at[i]).wait()
        carried[:, take] = mm(sigma[take, :], wide[...]).T.astype(BF)

    load_low.wait()
    load_high.wait()
    load_square.wait()
    step = 256
    for source, base in ((wide, me), (wide_other, 1 - me)):
        for c in range(half // step):
            put = pl.ds(pl.multiple_of(base * half + c * step, step), step)
            out[:, put] += mm(carried[...], source[:, pl.ds(c * step, step)])
            pltpu.make_async_copy(out.at[:, put], out_ref.at[:, put], store_sem).start()
    block_out = out[:, pl.ds(pl.multiple_of(me * half, half), half)]
    row = lax.broadcasted_iota(jnp.int32, (half, half), 0)
    col = lax.broadcasted_iota(jnp.int32, (half, half), 1)
    var_ref[...] = jnp.sum(jnp.where(row == col, block_out, 0.0), axis=0, keepdims=True)
    pltpu.make_async_copy(out, out_ref, store_sem).wait()


def on_device(sep_factor, coup_factor, coup_list, slot_tiles, anc_tiles):
    panels = lax.axis_size("panel")
    groups = lax.axis_size("front")
    half, width = sep_factor.shape
    edge = anc_tiles.shape[1]
    slots = slot_tiles.shape[1]
    strip_rows = anc_tiles.shape[0] // slots
    rows = coup_list.shape[1] * edge
    vmem = pl.BlockSpec(memory_space=pltpu.VMEM)
    smem = pl.BlockSpec(memory_space=pltpu.SMEM)
    hbm = pl.BlockSpec(memory_space=pltpu.HBM)
    depth = groups // 4
    dma = pltpu.SemaphoreType.DMA
    wide, wide_other, square, pool = pl.pallas_call(
        functools.partial(first_kernel, depth),
        out_shape=(
            jax.ShapeDtypeStruct((rows, half), BF),
            jax.ShapeDtypeStruct((rows, half), BF),
            jax.ShapeDtypeStruct((half, width), F32),
            jax.ShapeDtypeStruct((groups * anc_tiles.shape[0] + strip_rows, edge), BF),
        ),
        in_specs=[hbm] * 3,
        out_specs=[hbm] * 4,
        scratch_shapes=[
            pltpu.VMEM((width, width), BF),
            pltpu.VMEM((rows, half), BF),
            pltpu.VMEM((half, width), F32),
            pltpu.VMEM((width, width), BF),
            pltpu.VMEM((rows, width), BF),
            pltpu.VMEM((width, width), BF),
            pltpu.VMEM((width // DIAG, DIAG, DIAG), F32),
            dma((3,)),
            dma((3,)),
            dma((depth,)),
            dma((depth,)),
            dma((depth,)),
            dma((depth,)),
            dma((depth,)),
            dma,
            dma,
            dma((6,)),
        ],
        compiler_params=pltpu.CompilerParams(
            vmem_limit_bytes=48 << 20, collective_id=0, has_side_effects=True
        ),
    )(sep_factor, coup_factor, anc_tiles)
    selected, variances = pl.pallas_call(
        last_kernel,
        out_shape=(
            jax.ShapeDtypeStruct((half, width), F32),
            jax.ShapeDtypeStruct((1, half), F32),
        ),
        in_specs=[smem, smem] + [hbm] * 4,
        out_specs=[hbm, vmem],
        scratch_shapes=[
            pltpu.VMEM((rows, rows), BF),
            pltpu.VMEM((rows, half), BF),
            pltpu.VMEM((rows, half), BF),
            pltpu.VMEM((half, rows), BF),
            pltpu.VMEM((half, width), F32),
            pltpu.SMEM((groups * slots,), jnp.int32),
            dma((4,)),
            dma((4,)),
            dma,
        ],
        compiler_params=pltpu.CompilerParams(vmem_limit_bytes=48 << 20),
    )(coup_list, slot_tiles, wide, wide_other, square, pool)
    return selected, variances.reshape(half)


def solution(mesh):
    placed = (P(("front", "panel"), None), P(("front", "panel"), None), P(), P(), P("front", None))
    return jax.shard_map(
        on_device,
        mesh=mesh,
        in_specs=placed,
        out_specs=(P(("front", "panel"), None), P(("front", "panel"))),
        check_vma=False,
    )
```

```python
import functools

import jax
import jax.numpy as jnp
from jax import lax
from jax.experimental import pallas as pl
from jax.experimental.pallas import tpu as pltpu
from jax.sharding import PartitionSpec as P

BF = jnp.bfloat16
F32 = jnp.float32
DIAG = 128
MESH = pl.DeviceIdType.MESH


def mm(a, b):
    return jnp.dot(a, b, preferred_element_type=F32)


def split(x):
    hi = x.astype(BF)
    return hi, (x - hi.astype(F32)).astype(BF)


def flip(index, mask):
    bit = 1
    while bit <= mask:
        if mask & bit:
            index = index + bit * (1 - 2 * ((index // bit) % 2))
        bit *= 2
    return index


def first_kernel(
    depth,
    sep_ref,
    coup_ref,
    anc_ref,
    wide_out,
    wide_other,
    square_out,
    pool_ref,
    inv_ref,
    wide_ref,
    square_ref,
    lmat,
    coup_all,
    xl,
    xd,
    panel_send,
    panel_recv,
    z_recv,
    x_recv,
    y_recv,
    first_recv,
    second_recv,
    share_recv,
    out_send,
    local_sem,
):
    me = lax.axis_index("panel")
    group = lax.axis_index("front")
    layer, spot = group // 4, group % 4
    half, n = sep_ref.shape[0], sep_ref.shape[1]
    slab = anc_ref.shape[0]
    part = slab // 2
    partner = (group, 1 - me)
    beside = (layer * 4 + flip(spot, 1), me)
    behind = (layer * 4 + flip(spot, 2), me)
    peers = [(flip(layer, k) * 4 + spot, me) for k in range(1, depth)]

    barrier = pltpu.get_barrier_semaphore()
    for device in [partner, beside, behind] + peers:
        pl.semaphore_signal(barrier, inc=1, device_id=device, device_id_type=MESH)
    pl.semaphore_wait(barrier, 2 + depth)

    def remote(source, target, send, recv, device):
        return pltpu.make_async_remote_copy(
            src_ref=source, dst_ref=target, send_sem=send, recv_sem=recv, device_id=device, device_id_type=MESH
        )

    def place(k, mask, low=0, size=part):
        owner = flip(layer, k) * 4 + flip(spot, mask)
        start = pl.multiple_of(owner * slab + me * part + low, part // 2)
        return pool_ref.at[pl.ds(start, size), :]

    def push(source, target, recv, device):
        remote(source, target, out_send, recv, device).start()

    def arrived(target, recv):
        remote(target, target, out_send, recv, partner).wait_recv()

    own = anc_ref.at[pl.ds(pl.multiple_of(me * part, part), part), :]

    def open_block(k):
        source = own if k == 0 else place(k, 0)
        if k > 0:
            arrived(source, z_recv.at[k])
        push(source, place(k, 0), x_recv.at[k], beside)
        push(source, place(k, 0), y_recv.at[k], behind)
        if k > 0:
            push(source, source, share_recv, partner)

    def relay(k):
        piece = part // 2
        arrived(place(k, 1), x_recv.at[k])
        push(place(k, 1, piece, piece), place(k, 1, piece, piece), second_recv.at[k], behind)
        arrived(place(k, 2), y_recv.at[k])
        push(place(k, 2, 0, piece), place(k, 2, 0, piece), first_recv.at[k], beside)
        push(place(k, 1), place(k, 1), share_recv, partner)
        push(place(k, 2), place(k, 2), share_recv, partner)

    def finish(k):
        piece = part // 2
        arrived(place(k, 3, 0, piece), first_recv.at[k])
        arrived(place(k, 3, piece, piece), second_recv.at[k])
        push(place(k, 3), place(k, 3), share_recv, partner)

    def stage(k):
        if 2 <= k <= depth + 1:
            finish(k - 2)
        if 1 <= k <= depth:
            relay(k - 1)
        if k < depth:
            open_block(k)

    rows = coup_ref.shape[0]
    upper = pl.ds(pl.multiple_of(me * half, half), half)
    sep_copy = remote(sep_ref, lmat.at[upper, :], panel_send.at[0], panel_recv.at[0], partner)
    coup_copy = remote(coup_ref, coup_all.at[pl.ds(rows, rows), :], panel_send.at[1], panel_recv.at[1], partner)
    wide_copy = remote(wide_ref, wide_other, panel_send.at[2], panel_recv.at[2], partner)
    sep_keep = pltpu.make_async_copy(sep_ref, lmat.at[upper, :], local_sem.at[0])
    sep_copy.start()
    for k in range(1, depth):
        push(own, place(0, 0), z_recv.at[k], peers[k - 1])
        if k == 1:
            stage(0)
    coup_copy.start()
    sep_keep.start()
    coup_keep = pltpu.make_async_copy(coup_ref, coup_all.at[pl.ds(0, rows), :], local_sem.at[1])
    coup_keep.start()
    keep = pltpu.make_async_copy(
        anc_ref, pool_ref.at[pl.ds(pl.multiple_of(group * slab, slab), slab), :], local_sem.at[2]
    )
    keep.start()

    inv_ref[...] = jnp.zeros_like(inv_ref)
    xl[...] = jnp.zeros_like(xl)
    sep_keep.wait()
    remote(sep_ref, lmat.at[pl.ds(pl.multiple_of((1 - me) * half, half), half), :], panel_send.at[0], panel_recv.at[0], partner).wait_recv()

    blocks = n // DIAG
    row = lax.broadcasted_iota(jnp.int32, (DIAG, DIAG), 0)
    col = lax.broadcasted_iota(jnp.int32, (DIAG, DIAG), 1)
    eye = row == col
    for b in range(blocks):
        span = pl.ds(b * DIAG, DIAG)
        block = lmat[span, span].astype(F32)
        xd[b] = jnp.where(eye, 1.0 / jnp.where(eye, block, 1.0), 0.0)

    def level(step, carry):
        mask = (
            ((row >> (step + 1)) == (col >> (step + 1)))
            & (((row >> step) & 1) == 1)
            & (((col >> step) & 1) == 0)
        )
        for b in range(blocks):
            span = pl.ds(b * DIAG, DIAG)
            x = xd[b]
            hi, lo = split(x)
            below = jnp.where(mask, lmat[span, span].astype(F32), 0.0).astype(BF)
            y = mm(below, jnp.concatenate([hi, lo], axis=1))
            yhi, ylo = split(y[:, :DIAG] + y[:, DIAG:])
            t = mm(jnp.concatenate([hi, lo], axis=0), jnp.concatenate([yhi, ylo], axis=1))
            t = (t[:DIAG, :DIAG] + t[:DIAG, DIAG:]) + (t[DIAG:, :DIAG] + t[DIAG:, DIAG:])
            xd[b] = x - t
        return carry

    levels = DIAG.bit_length() - 1
    lax.fori_loop(0, levels // 2, level, 0)
    stage(1)
    lax.fori_loop(levels // 2, levels, level, 0)
    for b in range(blocks):
        span = pl.ds(b * DIAG, DIAG)
        inv_ref[span, span], xl[span, span] = split(xd[b])
    size = DIAG
    while size < n:
        for start in range(0, n, 2 * size):
            top, low = pl.ds(start, size), pl.ds(start + size, size)
            below = lmat[low, top]
            thi, tlo = split(mm(below, inv_ref[top, top]) + mm(below, xl[top, top]))
            t = mm(inv_ref[low, low], thi) + (mm(inv_ref[low, low], tlo) + mm(xl[low, low], thi))
            inv_ref[low, top], xl[low, top] = split(-t)
        size *= 2
    stage(2)

    chunk = min(512, rows)
    columns = pl.ds(pl.multiple_of(me * half, half), half)
    coup_keep.wait()
    coup_copy.wait_recv()

    @pl.loop(0, 2 * rows // chunk)
    def _(i):
        take = pl.ds(pl.multiple_of(i * chunk, chunk), chunk)
        wide_ref[take, :] = mm(coup_all[take, :], inv_ref[:, columns]).astype(BF)

    stage(3)
    wide_copy.start()
    wide_keep = pltpu.make_async_copy(wide_ref, wide_out, local_sem.at[3])
    wide_keep.start()
    strip = pool_ref.shape[0] - 4 * depth * slab
    blank = pltpu.make_async_copy(
        inv_ref.at[pl.ds(0, strip), pl.ds(n - DIAG, DIAG)], pool_ref.at[pl.ds(4 * depth * slab, strip), :], local_sem.at[4]
    )
    blank.start()

    @pl.loop(0, n // 256)
    def _(i):
        take = pl.ds(pl.multiple_of(i * 256, 256), 256)
        square_ref[:, take] = lax.dot_general(
            inv_ref[:, columns], inv_ref[:, take], (((0,), (0,)), ((), ())), preferred_element_type=F32
        )

    square_keep = pltpu.make_async_copy(square_ref, square_out, local_sem.at[5])
    square_keep.start()
    for k in range(4, depth + 2):
        stage(k)

    total = 4 * depth - 1
    shared = pool_ref.at[pl.ds(0, total * part), :]
    remote(shared, shared, out_send, share_recv, partner).wait_recv()
    sent = pool_ref.at[pl.ds(0, (2 * total) * part), :]
    remote(sent, sent, out_send, share_recv, partner).wait_send()
    for copy in (keep, wide_keep, blank, square_keep):
        copy.wait()
    sep_copy.wait_send()
    coup_copy.wait_send()
    wide_copy.wait()


def last_kernel(
    list_ref,
    slot_ref,
    wide_in,
    other_in,
    square_in,
    pool_ref,
    out_ref,
    var_ref,
    sigma,
    wide,
    wide_other,
    carried,
    out,
    place,
    tile_sem,
    load_sem,
    store_sem,
):
    me = lax.axis_index("panel")
    group = lax.axis_index("front")
    rows, half = wide.shape
    edge = pool_ref.shape[1]
    groups, slots = slot_ref.shape
    total = groups * slots
    strip_rows = rows * rows // (total * edge)
    strip_count = edge // strip_rows
    across = rows // edge
    chunks = tile_sem.shape[0]
    chunk = rows // chunks
    low, high = pl.ds(0, rows // 2), pl.ds(rows // 2, rows // 2)

    load_wide = pltpu.make_async_copy(wide_in, wide, load_sem.at[0])
    load_low = pltpu.make_async_copy(other_in.at[high, :], wide_other.at[low, :], load_sem.at[1])
    load_high = pltpu.make_async_copy(other_in.at[low, :], wide_other.at[high, :], load_sem.at[2])
    load_square = pltpu.make_async_copy(square_in, out, load_sem.at[3])
    load_wide.start()

    @pl.loop(0, groups)
    def _(g):
        for s in range(slots):
            place[slot_ref[g, s]] = g * slots + s

    def block(i):
        return list_ref[group, (i + me * (across // 2)) % across]

    def fetch(i):
        a = block(i)
        for j in range(across):
            b = block(j)
            live = (a >= 0) & (b >= 0)
            for q in range(strip_count):
                at = place[jnp.where(live, a * groups + b * strip_count + q, 0)]
                source = pl.multiple_of(jnp.where(live, at, total) * strip_rows, strip_rows)
                down = pl.multiple_of(i * edge + q * strip_rows, strip_rows)
                pltpu.make_async_copy(
                    pool_ref.at[pl.ds(source, strip_rows), :],
                    sigma.at[pl.ds(down, strip_rows), pl.ds(j * edge, edge)],
                    tile_sem.at[i // (across // chunks)],
                ).start()

    pl.loop(0, across)(fetch)
    load_low.start()
    load_high.start()
    load_square.start()
    load_wide.wait()

    @pl.loop(0, chunks)
    def _(i):
        take = pl.ds(pl.multiple_of(i * chunk, chunk), chunk)
        pltpu.make_async_copy(sigma.at[take, :], sigma.at[take, :], tile_sem.at[i]).wait()
        carried[:, take] = mm(sigma[take, :], wide[...]).T.astype(BF)

    load_low.wait()
    load_high.wait()
    load_square.wait()
    step = 256
    for source, base in ((wide, me), (wide_other, 1 - me)):
        for c in range(half // step):
            put = pl.ds(pl.multiple_of(base * half + c * step, step), step)
            out[:, put] += mm(carried[...], source[:, pl.ds(c * step, step)])
            pltpu.make_async_copy(out.at[:, put], out_ref.at[:, put], store_sem).start()
    block_out = out[:, pl.ds(pl.multiple_of(me * half, half), half)]
    row = lax.broadcasted_iota(jnp.int32, (half, half), 0)
    col = lax.broadcasted_iota(jnp.int32, (half, half), 1)
    var_ref[...] = jnp.sum(jnp.where(row == col, block_out, 0.0), axis=0, keepdims=True)
    pltpu.make_async_copy(out, out_ref, store_sem).wait()


def on_device(sep_factor, coup_factor, coup_list, slot_tiles, anc_tiles):
    panels = lax.axis_size("panel")
    groups = lax.axis_size("front")
    half, width = sep_factor.shape
    edge = anc_tiles.shape[1]
    slots = slot_tiles.shape[1]
    strip_rows = anc_tiles.shape[0] // slots
    rows = coup_list.shape[1] * edge
    vmem = pl.BlockSpec(memory_space=pltpu.VMEM)
    smem = pl.BlockSpec(memory_space=pltpu.SMEM)
    hbm = pl.BlockSpec(memory_space=pltpu.HBM)
    depth = groups // 4
    dma = pltpu.SemaphoreType.DMA
    wide, wide_other, square, pool = pl.pallas_call(
        functools.partial(first_kernel, depth),
        out_shape=(
            jax.ShapeDtypeStruct((rows, half), BF),
            jax.ShapeDtypeStruct((rows, half), BF),
            jax.ShapeDtypeStruct((half, width), F32),
            jax.ShapeDtypeStruct((groups * anc_tiles.shape[0] + strip_rows, edge), BF),
        ),
        in_specs=[hbm] * 3,
        out_specs=[hbm] * 4,
        scratch_shapes=[
            pltpu.VMEM((width, width), BF),
            pltpu.VMEM((rows, half), BF),
            pltpu.VMEM((half, width), F32),
            pltpu.VMEM((width, width), BF),
            pltpu.VMEM((rows, width), BF),
            pltpu.VMEM((width, width), BF),
            pltpu.VMEM((width // DIAG, DIAG, DIAG), F32),
            dma((3,)),
            dma((3,)),
            dma((depth,)),
            dma((depth,)),
            dma((depth,)),
            dma((depth,)),
            dma((depth,)),
            dma,
            dma,
            dma((6,)),
        ],
        compiler_params=pltpu.CompilerParams(
            vmem_limit_bytes=63 << 20, collective_id=0, has_side_effects=True
        ),
    )(sep_factor, coup_factor, anc_tiles)
    selected, variances = pl.pallas_call(
        last_kernel,
        out_shape=(
            jax.ShapeDtypeStruct((half, width), F32),
            jax.ShapeDtypeStruct((1, half), F32),
        ),
        in_specs=[smem, smem] + [hbm] * 4,
        out_specs=[hbm, vmem],
        scratch_shapes=[
            pltpu.VMEM((rows, rows), BF),
            pltpu.VMEM((rows, half), BF),
            pltpu.VMEM((rows, half), BF),
            pltpu.VMEM((half, rows), BF),
            pltpu.VMEM((half, width), F32),
            pltpu.SMEM((groups * slots,), jnp.int32),
            dma((4,)),
            dma((4,)),
            dma,
        ],
        compiler_params=pltpu.CompilerParams(vmem_limit_bytes=63 << 20),
    )(coup_list, slot_tiles, wide, wide_other, square, pool)
    return selected, variances.reshape(half)


def solution(mesh):
    placed = (P(("front", "panel"), None), P(("front", "panel"), None), P(), P(), P("front", None))
    return jax.shard_map(
        on_device,
        mesh=mesh,
        in_specs=placed,
        out_specs=(P(("front", "panel"), None), P(("front", "panel"))),
        check_vma=False,
    )
```

```python
import functools

import jax
import jax.numpy as jnp
from jax import lax
from jax.experimental import pallas as pl
from jax.experimental.pallas import tpu as pltpu
from jax.sharding import PartitionSpec as P

BF = jnp.bfloat16
F32 = jnp.float32
DIAG = 128
MESH = pl.DeviceIdType.MESH


def mm(a, b):
    return jnp.dot(a, b, preferred_element_type=F32)


def split(x):
    hi = x.astype(BF)
    return hi, (x - hi.astype(F32)).astype(BF)


def flip(index, mask):
    bit = 1
    while bit <= mask:
        if mask & bit:
            index = index + bit * (1 - 2 * ((index // bit) % 2))
        bit *= 2
    return index


def first_kernel(
    depth,
    sep_ref,
    coup_ref,
    anc_ref,
    wide_out,
    wide_other,
    square_out,
    pool_ref,
    inv_ref,
    wide_ref,
    square_ref,
    lmat,
    coup_all,
    xl,
    xd,
    panel_send,
    panel_recv,
    z_recv,
    x_recv,
    y_recv,
    first_recv,
    second_recv,
    share_recv,
    out_send,
    local_sem,
):
    me = lax.axis_index("panel")
    group = lax.axis_index("front")
    layer, spot = group // 4, group % 4
    half, n = sep_ref.shape[0], sep_ref.shape[1]
    slab = anc_ref.shape[0]
    part = slab // 2
    partner = (group, 1 - me)
    beside = (layer * 4 + flip(spot, 1), me)
    behind = (layer * 4 + flip(spot, 2), me)
    peers = [(flip(layer, k) * 4 + spot, me) for k in range(1, depth)]

    barrier = pltpu.get_barrier_semaphore()
    for device in [partner, beside, behind] + peers:
        pl.semaphore_signal(barrier, inc=1, device_id=device, device_id_type=MESH)
    pl.semaphore_wait(barrier, 2 + depth)

    def remote(source, target, send, recv, device):
        return pltpu.make_async_remote_copy(
            src_ref=source, dst_ref=target, send_sem=send, recv_sem=recv, device_id=device, device_id_type=MESH
        )

    def place(k, mask, low=0, size=part):
        owner = flip(layer, k) * 4 + flip(spot, mask)
        start = pl.multiple_of(owner * slab + me * part + low, part // 2)
        return pool_ref.at[pl.ds(start, size), :]

    def push(source, target, recv, device):
        remote(source, target, out_send, recv, device).start()

    def arrived(target, recv):
        remote(target, target, out_send, recv, partner).wait_recv()

    own = anc_ref.at[pl.ds(pl.multiple_of(me * part, part), part), :]

    def open_block(k):
        source = own if k == 0 else place(k, 0)
        if k > 0:
            arrived(source, z_recv.at[k])
        piece = part // 2
        for first in (True, False):
            for recv, device, low in (
                (x_recv, beside, piece if first else 0),
                (y_recv, behind, 0 if first else piece),
            ):
                push(
                    source.at[pl.ds(low, piece), :],
                    place(k, 0, low, piece),
                    recv.at[k if first else depth + k],
                    device,
                )
        if k > 0:
            push(source, source, share_recv, partner)

    def relay(k):
        piece = part // 2
        arrived(place(k, 1, piece, piece), x_recv.at[k])
        push(place(k, 1, piece, piece), place(k, 1, piece, piece), second_recv.at[k], behind)
        arrived(place(k, 2, 0, piece), y_recv.at[k])
        push(place(k, 2, 0, piece), place(k, 2, 0, piece), first_recv.at[k], beside)
        arrived(place(k, 1, 0, piece), x_recv.at[depth + k])
        arrived(place(k, 2, piece, piece), y_recv.at[depth + k])
        push(place(k, 1), place(k, 1), share_recv, partner)
        push(place(k, 2), place(k, 2), share_recv, partner)

    def finish(k):
        piece = part // 2
        arrived(place(k, 3, 0, piece), first_recv.at[k])
        arrived(place(k, 3, piece, piece), second_recv.at[k])
        push(place(k, 3), place(k, 3), share_recv, partner)

    def stage(k):
        if 2 <= k <= depth + 1:
            finish(k - 2)
        if 1 <= k <= depth:
            relay(k - 1)
        if k < depth:
            open_block(k)

    rows = coup_ref.shape[0]
    upper = pl.ds(pl.multiple_of(me * half, half), half)
    sep_copy = remote(sep_ref, lmat.at[upper, :], panel_send.at[0], panel_recv.at[0], partner)
    coup_copy = remote(coup_ref, coup_all.at[pl.ds(rows, rows), :], panel_send.at[1], panel_recv.at[1], partner)
    wide_copy = remote(wide_ref, wide_other, panel_send.at[2], panel_recv.at[2], partner)
    sep_keep = pltpu.make_async_copy(sep_ref, lmat.at[upper, :], local_sem.at[0])
    sep_copy.start()
    for k in range(1, depth):
        push(own, place(0, 0), z_recv.at[k], peers[k - 1])
        if k == 1:
            stage(0)
    coup_copy.start()
    sep_keep.start()
    coup_keep = pltpu.make_async_copy(coup_ref, coup_all.at[pl.ds(0, rows), :], local_sem.at[1])
    coup_keep.start()
    keep = pltpu.make_async_copy(
        anc_ref, pool_ref.at[pl.ds(pl.multiple_of(group * slab, slab), slab), :], local_sem.at[2]
    )
    keep.start()

    inv_ref[...] = jnp.zeros_like(inv_ref)
    xl[...] = jnp.zeros_like(xl)
    sep_keep.wait()
    remote(sep_ref, lmat.at[pl.ds(pl.multiple_of((1 - me) * half, half), half), :], panel_send.at[0], panel_recv.at[0], partner).wait_recv()

    blocks = n // DIAG
    row = lax.broadcasted_iota(jnp.int32, (DIAG, DIAG), 0)
    col = lax.broadcasted_iota(jnp.int32, (DIAG, DIAG), 1)
    eye = row == col
    for b in range(blocks):
        span = pl.ds(b * DIAG, DIAG)
        block = lmat[span, span].astype(F32)
        xd[b] = jnp.where(eye, 1.0 / jnp.where(eye, block, 1.0), 0.0)

    def level(step, carry):
        mask = (
            ((row >> (step + 1)) == (col >> (step + 1)))
            & (((row >> step) & 1) == 1)
            & (((col >> step) & 1) == 0)
        )
        for b in range(blocks):
            span = pl.ds(b * DIAG, DIAG)
            x = xd[b]
            hi, lo = split(x)
            below = jnp.where(mask, lmat[span, span].astype(F32), 0.0).astype(BF)
            y = mm(below, jnp.concatenate([hi, lo], axis=1))
            yhi, ylo = split(y[:, :DIAG] + y[:, DIAG:])
            t = mm(jnp.concatenate([hi, lo], axis=0), jnp.concatenate([yhi, ylo], axis=1))
            t = (t[:DIAG, :DIAG] + t[:DIAG, DIAG:]) + (t[DIAG:, :DIAG] + t[DIAG:, DIAG:])
            xd[b] = x - t
        return carry

    levels = DIAG.bit_length() - 1
    lax.fori_loop(0, levels // 2, level, 0)
    stage(1)
    lax.fori_loop(levels // 2, levels, level, 0)
    for b in range(blocks):
        span = pl.ds(b * DIAG, DIAG)
        inv_ref[span, span], xl[span, span] = split(xd[b])
    size = DIAG
    while size < n:
        for start in range(0, n, 2 * size):
            top, low = pl.ds(start, size), pl.ds(start + size, size)
            below = lmat[low, top]
            thi, tlo = split(mm(below, inv_ref[top, top]) + mm(below, xl[top, top]))
            t = mm(inv_ref[low, low], thi) + (mm(inv_ref[low, low], tlo) + mm(xl[low, low], thi))
            inv_ref[low, top], xl[low, top] = split(-t)
        size *= 2
    stage(2)

    chunk = min(512, rows)
    columns = pl.ds(pl.multiple_of(me * half, half), half)
    coup_keep.wait()
    coup_copy.wait_recv()

    @pl.loop(0, 2 * rows // chunk)
    def _(i):
        take = pl.ds(pl.multiple_of(i * chunk, chunk), chunk)
        wide_ref[take, :] = mm(coup_all[take, :], inv_ref[:, columns]).astype(BF)

    stage(3)
    wide_copy.start()
    wide_keep = pltpu.make_async_copy(wide_ref, wide_out, local_sem.at[3])
    wide_keep.start()
    strip = pool_ref.shape[0] - 4 * depth * slab
    blank = pltpu.make_async_copy(
        inv_ref.at[pl.ds(0, strip), pl.ds(n - DIAG, DIAG)], pool_ref.at[pl.ds(4 * depth * slab, strip), :], local_sem.at[4]
    )
    blank.start()

    @pl.loop(0, n // 256)
    def _(i):
        take = pl.ds(pl.multiple_of(i * 256, 256), 256)
        square_ref[:, take] = lax.dot_general(
            inv_ref[:, columns], inv_ref[:, take], (((0,), (0,)), ((), ())), preferred_element_type=F32
        )

    square_keep = pltpu.make_async_copy(square_ref, square_out, local_sem.at[5])
    square_keep.start()
    for k in range(4, depth + 2):
        stage(k)

    total = 4 * depth - 1
    shared = pool_ref.at[pl.ds(0, total * part), :]
    remote(shared, shared, out_send, share_recv, partner).wait_recv()
    sent = pool_ref.at[pl.ds(0, (2 * total) * part), :]
    remote(sent, sent, out_send, share_recv, partner).wait_send()
    for copy in (keep, wide_keep, blank, square_keep):
        copy.wait()
    sep_copy.wait_send()
    coup_copy.wait_send()
    wide_copy.wait()


def last_kernel(
    list_ref,
    slot_ref,
    wide_in,
    other_in,
    square_in,
    pool_ref,
    out_ref,
    var_ref,
    sigma,
    wide,
    wide_other,
    carried,
    out,
    place,
    tile_sem,
    load_sem,
    store_sem,
):
    me = lax.axis_index("panel")
    group = lax.axis_index("front")
    rows, half = wide.shape
    edge = pool_ref.shape[1]
    groups, slots = slot_ref.shape
    total = groups * slots
    strip_rows = rows * rows // (total * edge)
    strip_count = edge // strip_rows
    across = rows // edge
    chunks = tile_sem.shape[0]
    chunk = rows // chunks
    low, high = pl.ds(0, rows // 2), pl.ds(rows // 2, rows // 2)

    load_wide = pltpu.make_async_copy(wide_in, wide, load_sem.at[0])
    load_low = pltpu.make_async_copy(other_in.at[high, :], wide_other.at[low, :], load_sem.at[1])
    load_high = pltpu.make_async_copy(other_in.at[low, :], wide_other.at[high, :], load_sem.at[2])
    load_square = pltpu.make_async_copy(square_in, out, load_sem.at[3])
    load_wide.start()

    @pl.loop(0, groups)
    def _(g):
        for s in range(slots):
            place[slot_ref[g, s]] = g * slots + s

    def block(i):
        return list_ref[group, (i + me * (across // 2)) % across]

    def fetch(i):
        a = block(i)
        for j in range(across):
            b = block(j)
            live = (a >= 0) & (b >= 0)
            for q in range(strip_count):
                at = place[jnp.where(live, a * groups + b * strip_count + q, 0)]
                source = pl.multiple_of(jnp.where(live, at, total) * strip_rows, strip_rows)
                down = pl.multiple_of(i * edge + q * strip_rows, strip_rows)
                pltpu.make_async_copy(
                    pool_ref.at[pl.ds(source, strip_rows), :],
                    sigma.at[pl.ds(down, strip_rows), pl.ds(j * edge, edge)],
                    tile_sem.at[i // (across // chunks)],
                ).start()

    pl.loop(0, across)(fetch)
    load_low.start()
    load_high.start()
    load_square.start()
    load_wide.wait()

    @pl.loop(0, chunks)
    def _(i):
        take = pl.ds(pl.multiple_of(i * chunk, chunk), chunk)
        pltpu.make_async_copy(sigma.at[take, :], sigma.at[take, :], tile_sem.at[i]).wait()
        carried[:, take] = mm(sigma[take, :], wide[...]).T.astype(BF)

    load_low.wait()
    load_high.wait()
    load_square.wait()
    step = 256
    for source, base in ((wide, me), (wide_other, 1 - me)):
        for c in range(half // step):
            put = pl.ds(pl.multiple_of(base * half + c * step, step), step)
            out[:, put] += mm(carried[...], source[:, pl.ds(c * step, step)])
            pltpu.make_async_copy(out.at[:, put], out_ref.at[:, put], store_sem).start()
    block_out = out[:, pl.ds(pl.multiple_of(me * half, half), half)]
    row = lax.broadcasted_iota(jnp.int32, (half, half), 0)
    col = lax.broadcasted_iota(jnp.int32, (half, half), 1)
    var_ref[...] = jnp.sum(jnp.where(row == col, block_out, 0.0), axis=0, keepdims=True)
    pltpu.make_async_copy(out, out_ref, store_sem).wait()


def on_device(sep_factor, coup_factor, coup_list, slot_tiles, anc_tiles):
    panels = lax.axis_size("panel")
    groups = lax.axis_size("front")
    half, width = sep_factor.shape
    edge = anc_tiles.shape[1]
    slots = slot_tiles.shape[1]
    strip_rows = anc_tiles.shape[0] // slots
    rows = coup_list.shape[1] * edge
    vmem = pl.BlockSpec(memory_space=pltpu.VMEM)
    smem = pl.BlockSpec(memory_space=pltpu.SMEM)
    hbm = pl.BlockSpec(memory_space=pltpu.HBM)
    depth = groups // 4
    dma = pltpu.SemaphoreType.DMA
    wide, wide_other, square, pool = pl.pallas_call(
        functools.partial(first_kernel, depth),
        out_shape=(
            jax.ShapeDtypeStruct((rows, half), BF),
            jax.ShapeDtypeStruct((rows, half), BF),
            jax.ShapeDtypeStruct((half, width), F32),
            jax.ShapeDtypeStruct((groups * anc_tiles.shape[0] + strip_rows, edge), BF),
        ),
        in_specs=[hbm] * 3,
        out_specs=[hbm] * 4,
        scratch_shapes=[
            pltpu.VMEM((width, width), BF),
            pltpu.VMEM((rows, half), BF),
            pltpu.VMEM((half, width), F32),
            pltpu.VMEM((width, width), BF),
            pltpu.VMEM((rows, width), BF),
            pltpu.VMEM((width, width), BF),
            pltpu.VMEM((width // DIAG, DIAG, DIAG), F32),
            dma((3,)),
            dma((3,)),
            dma((depth,)),
            dma((2 * depth,)),
            dma((2 * depth,)),
            dma((depth,)),
            dma((depth,)),
            dma,
            dma,
            dma((6,)),
        ],
        compiler_params=pltpu.CompilerParams(
            vmem_limit_bytes=63 << 20, collective_id=0, has_side_effects=True
        ),
    )(sep_factor, coup_factor, anc_tiles)
    selected, variances = pl.pallas_call(
        last_kernel,
        out_shape=(
            jax.ShapeDtypeStruct((half, width), F32),
            jax.ShapeDtypeStruct((1, half), F32),
        ),
        in_specs=[smem, smem] + [hbm] * 4,
        out_specs=[hbm, vmem],
        scratch_shapes=[
            pltpu.VMEM((rows, rows), BF),
            pltpu.VMEM((rows, half), BF),
            pltpu.VMEM((rows, half), BF),
            pltpu.VMEM((half, rows), BF),
            pltpu.VMEM((half, width), F32),
            pltpu.SMEM((groups * slots,), jnp.int32),
            dma((4,)),
            dma((4,)),
            dma,
        ],
        compiler_params=pltpu.CompilerParams(vmem_limit_bytes=63 << 20),
    )(coup_list, slot_tiles, wide, wide_other, square, pool)
    return selected, variances.reshape(half)


def solution(mesh):
    placed = (P(("front", "panel"), None), P(("front", "panel"), None), P(), P(), P("front", None))
    return jax.shard_map(
        on_device,
        mesh=mesh,
        in_specs=placed,
        out_specs=(P(("front", "panel"), None), P(("front", "panel"))),
        check_vma=False,
    )
```
